32 devices in a mesh: frames: 4 (over y, x), rows: 8 (over z, core).
Axes of the slice: x: 2, y: 2, z: 4, core: 2. Of those that a mesh axis runs over, the one named last changes fastest.
Arguments:
- inputs: bfloat16 [4, 32, 424, 256], P('frames', 'rows'), may hold values from -350 to 350, as said below
- cotangent: bfloat16 [4, 32, 424, 256], P('frames', 'rows'), may hold values from -140 to 140, as said below
- kernel: bfloat16 [3, 3, 3, 256, 256], replicated, may hold values from -0.078125 to 0.078125
- norm_gain: float32 [256], replicated, may hold values from 0.1 to 1.9
- norm_bias: float32 [256], replicated, may hold values from -1 to 1
Outputs:
- input_grad: bfloat16 [4, 32, 424, 256], P('frames', 'rows')
The draws below stay inside these ranges and needn't reach their ends.
Inputs may be any that keep to these rules, and one draw needn't show every extreme that they name: `inputs`: finite values. `cotangent`: finite values.
All inputs are finite; a program needn't handle non-finite values.
Results may differ from the reference program's by a relative error of at most 0.0055.
Values may be sent and summed in bfloat16 or wider, within the bound.
No kernel may reach another device: no remote copies, remote signals or barrier semaphores. Data moves between devices by JAX's collectives and lax.ppermute only.
A program may use at most 64 MiB of HBM per device.

```python
import math
import jax
import jax.numpy as jnp
from jax import lax

C = 256
GROUPS = 32
WIDTH = 424
HEIGHT = 32
FRAMES = 4


def frame_factors():
    steps = jnp.arange(FRAMES, dtype=jnp.float32)
    factor = (1.0 + 0.5 * steps) / (1.0 + 0.5 * (FRAMES - 1))
    shift = 1.5 * (2.0 * steps / max(FRAMES - 1, 1) - 1.0)
    return (factor, shift)


def draw_inputs(key, part):
    keys = jax.random.split(jax.random.fold_in(key, 11), 4)
    shape = (FRAMES, HEIGHT, WIDTH, C)
    rows = jnp.arange(HEIGHT, dtype=jnp.float32) / max(HEIGHT - 1, 1)
    chan_scale = jnp.exp(jax.random.uniform(keys[1], (C,), jnp.float32, 0.0, math.log(10.0)))
    col_scale = jnp.exp(jax.random.uniform(keys[2], (WIDTH,), jnp.float32, 0.0, math.log(3.0)))
    offset = jax.random.uniform(keys[3], (C,), jnp.float32, -2.0, 2.0)
    factor, shift = frame_factors()
    noise = jnp.clip(jax.random.normal(keys[0], shape, jnp.float32), -4.0, 4.0)
    row_scale = 3.0 ** rows
    spread = noise * row_scale[:, None, None] * col_scale[:, None] * factor[:, None, None, None]
    values = offset + (spread + shift[:, None, None, None]) * chan_scale / 3.0
    return values.astype(jnp.bfloat16)


def draw_cotangent(key, part):
    keys = jax.random.split(jax.random.fold_in(key, 23), 4)
    shape = (FRAMES, HEIGHT, WIDTH, C)
    rows = jnp.arange(HEIGHT, dtype=jnp.float32) / max(HEIGHT - 1, 1)
    chan_scale = jnp.exp(jax.random.uniform(keys[1], (C,), jnp.float32, 0.0, math.log(4.0)))
    col_scale = jnp.exp(jax.random.uniform(keys[2], (WIDTH,), jnp.float32, 0.0, math.log(3.0)))
    offset = jax.random.uniform(keys[3], (C,), jnp.float32, -1.0, 1.0)
    factor, shift = frame_factors()
    noise = jnp.clip(jax.random.normal(keys[0], shape, jnp.float32), -4.0, 4.0)
    row_scale = 3.0 ** rows
    values = offset + noise * row_scale[:, None, None] * col_scale[:, None] * chan_scale / 3.0
    values = values * factor[:, None, None, None]
    return values.astype(jnp.bfloat16)


def gaussian(own_key, shape, deviation, limit, held_as=jnp.bfloat16):
    result = jax.random.normal(own_key, shape, jnp.float32) * deviation
    return jnp.minimum(jnp.maximum(result, -limit), limit).astype(held_as)


def setup_inputs(seed: int = 0) -> dict:
    streams_of = jax.random.split(jax.random.key(seed), 6)
    return {
        "inputs": draw_inputs(jax.random.fold_in(streams_of[5], 71), 0),
        "cotangent": draw_cotangent(jax.random.fold_in(streams_of[5], 71), 0),
        "kernel": gaussian(streams_of[2], (3, 3, 3, C, C), (27 * C) ** -0.5, 0.078125),
        "norm_gain": jnp.clip(1.0 + 0.18 * jax.random.normal(streams_of[3], (C,), jnp.float32), 0.1, 1.9),
        "norm_bias": jnp.clip(jax.random.uniform(streams_of[4], (C,), jnp.float32, -1.0, 1.0), -1.0, 1.0),
    }


EPS = 1e-06

def group_sum(values):
    per_chan = lax.optimization_barrier(jnp.sum(values, axis=(0, 1, 2)))
    return lax.optimization_barrier(jnp.sum(per_chan.reshape(GROUPS, -1), axis=1))

def spread_groups(per_group, channels):
    return jnp.repeat(per_group, channels // GROUPS)

def reference(inputs, cotangent, kernel, norm_gain, norm_bias):
    values = inputs.astype(jnp.float32)
    channels = values.shape[-1]
    cells_per = values.shape[0] * values.shape[1] * values.shape[2] * (channels // GROUPS)
    centre = group_sum(values) / cells_per
    centred = values - spread_groups(centre, channels)
    variance = group_sum(centred * centred) / cells_per
    inv_std = spread_groups(lax.rsqrt(variance + EPS), channels)
    normed = centred * inv_std
    preact = normed * norm_gain + norm_bias
    weights = kernel.astype(jnp.float32)

    def forward(active):
        return lax.conv_general_dilated(active[None], weights, (1, 1, 1), ((2, 0), (1, 1), (1, 1)), dimension_numbers=('NDHWC', 'DHWIO', 'NDHWC'), precision=lax.Precision.HIGHEST)[0]
    _, pullback = jax.vjp(forward, jnp.zeros_like(values))
    act_grad = pullback(cotangent.astype(jnp.float32))[0]
    logistic = jax.nn.sigmoid(preact)
    norm_grad = act_grad * logistic * (1.0 + preact * (1.0 - logistic)) * norm_gain
    grad_total = group_sum(norm_grad) / cells_per
    grad_cross = group_sum(norm_grad * normed) / cells_per
    input_grad = inv_std * (norm_grad - spread_groups(grad_total, channels) - normed * spread_groups(grad_cross, channels))
    return input_grad.astype(jnp.bfloat16)
```

```python
import functools
import jax
import jax.numpy as jnp
from jax import lax
from jax.experimental import pallas as pl
from jax.experimental.pallas import tpu as pltpu
from jax.sharding import PartitionSpec as P

GROUPS = 32
EPS = 1e-06
F32 = jnp.float32
BF16 = jnp.bfloat16
HIGH = lax.Precision.HIGHEST
VMEM = pl.BlockSpec(memory_space=pltpu.VMEM)
LIMIT = 60 * 1024 * 1024


def call(body, out_shape, flops, moved, in_specs=None, **kw):
    return pl.pallas_call(
        body,
        out_shape=out_shape,
        cost_estimate=pl.CostEstimate(flops=flops, bytes_accessed=moved, transcendentals=0),
        compiler_params=pltpu.CompilerParams(vmem_limit_bytes=LIMIT),
        **({} if in_specs is None else {"in_specs": in_specs}),
        **kw,
    )


def membership(channels, lanes, flip):
    per = channels // GROUPS
    shape = (lanes, channels) if flip else (channels, lanes)
    chan = lax.broadcasted_iota(jnp.int32, shape, 1 if flip else 0)
    lane = lax.broadcasted_iota(jnp.int32, shape, 0 if flip else 1)
    return (chan // per == lane).astype(F32)


def pack_sums(first, second, out_ref):
    channels = first.shape[-1]
    row = lax.broadcasted_iota(jnp.int32, (8, channels), 0)
    both = jnp.where(row == 0, first, jnp.where(row == 1, second, 0.0))
    sums = jnp.dot(both, membership(channels, 128, False), precision=HIGH, preferred_element_type=F32)
    out_ref[...] = jnp.broadcast_to(sums[None], out_ref.shape)


def unpack_sums(got_ref, channels, cells):
    total = jnp.sum(got_ref[...], axis=0) / cells
    wide = jnp.dot(total, membership(channels, 128, True), precision=HIGH, preferred_element_type=F32)
    return wide, total


def stats_body(x_ref, out_ref):
    v = x_ref[0].astype(F32)
    v = v.reshape(-1, v.shape[-1])
    pack_sums(jnp.sum(v, axis=0, keepdims=True), jnp.sum(v * v, axis=0, keepdims=True), out_ref)


def norm_params(got_ref, channels, cells):
    total = jnp.sum(got_ref[...], axis=0) / cells
    centre, square = total[0:1], total[1:2]
    variance = jnp.maximum(square - centre * centre, 0.0)
    inv_std = lax.rsqrt(variance + EPS)
    row = lax.broadcasted_iota(jnp.int32, (8, 128), 0)
    both = jnp.where(row == 0, centre, jnp.where(row == 1, inv_std, 0.0))
    wide = jnp.dot(both, membership(channels, 128, True), precision=HIGH, preferred_element_type=F32)
    return wide[0:1], wide[1:2]


def taps(lhs, w):
    return lax.dot_general(lhs, w, (((1,), (1,)), ((), ())), preferred_element_type=F32)


def columns(a):
    width, wide = a.shape
    c = wide // 3
    at = lax.broadcasted_iota(jnp.int32, (width, c), 0)
    left = pltpu.roll(a[:, :c], width - 1, 0)
    right = pltpu.roll(a[:, 2 * c :], 1, 0)
    left = jnp.where(at == width - 1, 0.0, left)
    right = jnp.where(at == 0, 0.0, right)
    return a[:, c : 2 * c] + left + right


def weights(w_ref, row_tap, frame_taps):
    c = w_ref.shape[-1]
    parts = [w_ref[k, row_tap].reshape(3 * c, c) for k in frame_taps]
    return parts[0] if len(parts) == 1 else jnp.concatenate(parts, axis=1)


def own_body(f_ref, w_ref, acc_ref):
    _, strip, width, c = f_ref.shape
    ws = [w_ref[0, i].reshape(3 * c, c) for i in range(3)]
    for y in range(-1, strip + 1):
        rows = [(y + 1 - i, i) for i in range(3) if 0 <= y + 1 - i < strip]
        lhs = jnp.concatenate([f_ref[0, r] for r, _ in rows], axis=1)
        w = jnp.concatenate([ws[i] for _, i in rows], axis=1)
        acc_ref[y + 1] = columns(taps(lhs, w))


def border_body(xl_ref, dl_ref, lt_ref, w_ref, acc_ref, out_ref, up_ref, down_ref):
    strip, width, c = xl_ref.shape
    ends = (0, strip - 1)
    lhs = [
        jnp.concatenate([xl_ref[r] + dl_ref[n], lt_ref[n]], axis=1) for n, r in enumerate(ends)
    ]
    for i in range(3):
        w = jnp.concatenate([w_ref[1, i].reshape(3 * c, c), w_ref[0, i].reshape(3 * c, c)], axis=1)
        for n, r in enumerate(ends):
            y = r - 1 + i
            value = acc_ref[y + 1] + columns(taps(lhs[n], w))
            if y == -1:
                up_ref[...] = value.astype(BF16)
            elif y == strip:
                down_ref[...] = value.astype(BF16)
            else:
                out_ref[y] = value


def inner_conv(rows, w_ref, acc, strip, put):
    c = w_ref.shape[-1]
    ws = [w_ref[0, i].reshape(3 * c, c) for i in range(3)]
    for y in range(strip):
        use = [(y + 1 - i, i) for i in range(3) if 1 <= y + 1 - i < strip - 1]
        lhs = jnp.concatenate([rows[r - 1] for r, _ in use], axis=1)
        w = jnp.concatenate([ws[i] for _, i in use], axis=1)
        put(y, acc[y] + columns(taps(lhs, w)))


def inner_body(xl_ref, rl_ref, w_ref, acc_ref, out_ref):
    strip = acc_ref.shape[0]
    rows = [xl_ref[r] + rl_ref[r - 1] for r in range(1, strip - 1)]

    def put(y, value):
        out_ref[y] = value

    inner_conv(rows, w_ref, acc_ref, strip, put)


def last_body(
    cells, a_ref, b_ref, w_ref, acc_ref, above_ref, below_ref, x_ref, got_ref, gain_ref, bias_ref,
    grad_ref, sums_ref,
):
    strip, _, c = acc_ref.shape
    rows = [a_ref[r] + b_ref[r] for r in range(strip - 2)]
    centre, inv_std = norm_params(got_ref, c, cells)
    gain, bias = gain_ref[...], bias_ref[...]
    sums = [jnp.zeros((1, c), F32), jnp.zeros((1, c), F32)]

    def put(y, value):
        if y == 0:
            value = value + above_ref[...].astype(F32)
        if y == strip - 1:
            value = value + below_ref[...].astype(F32)
        normed = (x_ref[0, y].astype(F32) - centre) * inv_std
        preact = normed * gain + bias
        logistic = jax.nn.sigmoid(preact)
        grad = value * logistic * (1.0 + preact * (1.0 - logistic)) * gain
        grad_ref[y] = grad
        sums[0] = sums[0] + jnp.sum(grad, axis=0, keepdims=True)
        sums[1] = sums[1] + jnp.sum(grad * normed, axis=0, keepdims=True)

    inner_conv(rows, w_ref, acc_ref, strip, put)
    pack_sums(sums[0], sums[1], sums_ref)


def final_body(cells, grad_ref, x_ref, got_ref, sums_ref, out_ref):
    strip, _, c = grad_ref.shape
    centre, inv_std = norm_params(got_ref, c, cells)
    wide, _ = unpack_sums(sums_ref, c, cells)
    total, cross = wide[0:1], wide[1:2]
    for y in range(strip):
        normed = (x_ref[0, y].astype(F32) - centre) * inv_std
        value = inv_std * (grad_ref[y] - total - normed * cross)
        out_ref[0, y] = value.astype(BF16)


def shards(inputs, cotangent, kernel, norm_gain, norm_bias):
    _, strip, width, c = inputs.shape
    frames, lines = lax.axis_size("frames"), lax.axis_size("rows")
    devices = frames * lines
    cells = float(devices * strip * width * (c // GROUPS))
    slab = cotangent[0]
    inner = slab[1 : strip - 1]
    ends = jnp.concatenate([slab[:1], slab[strip - 1 :]])

    def move(value, pairs):
        return lax.ppermute(value, "frames", pairs)

    def two(keep):
        return [(i, i - 2) for i in range(2, frames) if keep(i)]

    even, odd = (lambda i: i % 2 == 0), (lambda i: i % 2 == 1)
    later_x = move(slab, [(i, i - 1) for i in range(1, frames, 2)])
    latest_in_even = move(inner, two(even))
    later_ends = move(ends, [(i, i - 1) for i in range(2, frames, 2)])
    latest_ends = move(ends, two(lambda i: True))
    latest_in_odd = move(inner, two(odd))
    later_in = move(latest_in_even, [(i, i + 1) for i in range(0, frames - 2, 2)])

    row_f32 = jax.ShapeDtypeStruct((strip, width, c), F32)
    row_b16 = jax.ShapeDtypeStruct((width, c), BF16)
    sums_shape = jax.ShapeDtypeStruct((devices, 8, 128), F32)
    tap = 2 * width * c * c * 3
    size = width * c

    def swap(sums):
        return lax.all_to_all(sums, ("frames", "rows"), 0, 0, tiled=True)

    got = swap(call(stats_body, sums_shape, 8 * strip * size, 2 * strip * size)(inputs))

    def kspec(start, count):
        return pl.BlockSpec((count, 3, 3, c, c), lambda g: (start // count, 0, 0, 0, 0))

    def full(shape):
        return pl.BlockSpec(shape, lambda g: (0,) * len(shape))

    def conv_call(body, shapes, out_shapes, wspec, at, flops, moved):
        specs = [full(s) for s in shapes]
        specs.insert(at, wspec)
        one = not isinstance(out_shapes, (list, tuple))
        outs = full(out_shapes.shape) if one else [full(o.shape) for o in out_shapes]
        return call(
            body, out_shapes, flops, moved, in_specs=specs, out_specs=outs, grid=(1,)
        )

    acc6 = jax.ShapeDtypeStruct((strip + 2, width, c), F32)
    whole, pair, line = (strip, width, c), (strip - 2, width, c), (width, c)
    own = conv_call(own_body, [cotangent.shape], acc6, kspec(2, 1), 1, tap * 3 * strip, 8 * 6 * size)(
        cotangent, kernel
    )
    acc, up, down = conv_call(
        border_body, [whole, (2, width, c), (2, width, c), acc6.shape], [row_f32, row_b16, row_b16],
        kspec(0, 2), 3, tap * 12, 8 * 16 * size,
    )(later_x, later_ends, latest_ends, kernel, own)
    to_next = [(i, i + 1) for i in range(lines - 1)]
    to_prev = [(i + 1, i) for i in range(lines - 1)]
    above = lax.ppermute(down, "rows", to_next)
    below = lax.ppermute(up, "rows", to_prev)
    acc = conv_call(inner_body, [whole, pair, whole], row_f32, kspec(1, 1), 2, tap * 6, 8 * 12 * size)(
        later_x, later_in, kernel, acc
    )
    vec = norm_gain.reshape(1, c), norm_bias.reshape(1, c)
    grad, sums = conv_call(
        functools.partial(last_body, cells),
        [pair, pair, whole, line, line, inputs.shape, sums_shape.shape, (1, c), (1, c)],
        [row_f32, sums_shape], kspec(0, 1), 2, tap * 6, 8 * 12 * size,
    )(latest_in_even, latest_in_odd, kernel, acc, above, below, inputs, got, *vec)
    sums = swap(sums)
    return call(
        functools.partial(final_body, cells), jax.ShapeDtypeStruct(inputs.shape, BF16),
        10 * strip * size, 8 * strip * size,
    )(grad, inputs, got, sums)


def solution(mesh):
    return jax.shard_map(
        shards,
        mesh=mesh,
        in_specs=(P("frames", "rows", None, None), P("frames", "rows", None, None), P(), P(), P()),
        out_specs=P("frames", "rows", None, None),
        check_vma=False,
    )
```

```python
import functools
import jax
import jax.numpy as jnp
from jax import lax
from jax.experimental import pallas as pl
from jax.experimental.pallas import tpu as pltpu
from jax.sharding import PartitionSpec as P

GROUPS = 32
EPS = 1e-06
F32 = jnp.float32
BF16 = jnp.bfloat16
HIGH = lax.Precision.HIGHEST
DMA = pltpu.SemaphoreType.DMA
LIMIT = 24 * 1024 * 1024


def call(body, outs, flops, moved, args, near=(), far=(), scratch=()):
    spaces = [pltpu.VMEM if n in near else pltpu.HBM if n in far else None for n in range(len(args))]
    return pl.pallas_call(
        body,
        out_shape=outs,
        in_specs=[pl.BlockSpec(memory_space=m or pl.ANY) for m in spaces],
        out_specs=[
            pl.BlockSpec(memory_space=pltpu.HBM if isinstance(o, jax.ShapeDtypeStruct) else pltpu.VMEM)
            for o in outs
        ],
        scratch_shapes=list(scratch),
        cost_estimate=pl.CostEstimate(flops=flops, bytes_accessed=moved, transcendentals=0),
        compiler_params=pltpu.CompilerParams(vmem_limit_bytes=LIMIT),
    )(*(v if m is None else pltpu.with_memory_space_constraint(v, m) for v, m in zip(args, spaces)))


def fetch(sems, *pairs):
    copies = [pltpu.make_async_copy(a, b, sems.at[n]) for n, (a, b) in enumerate(pairs)]
    for copy in copies:
        copy.start()
    return copies


def same_group(channels):
    per = channels // GROUPS
    one = lax.broadcasted_iota(jnp.int32, (channels, channels), 0) // per
    two = lax.broadcasted_iota(jnp.int32, (channels, channels), 1) // per
    return (one == two).astype(F32)


def pack_sums(first, second, out_ref):
    channels = first.shape[-1]
    row = lax.broadcasted_iota(jnp.int32, (8, channels), 0)
    both = jnp.where(row == 0, first, jnp.where(row == 1, second, 0.0))
    sums = jnp.dot(both, same_group(channels), precision=HIGH, preferred_element_type=F32)
    out_ref[...] = jnp.broadcast_to(sums[None, 0:2], out_ref.shape)


def stats_body(x_ref, out_ref, near, sems):
    _, strip, _, c = x_ref.shape
    copies = fetch(sems, *((x_ref.at[0, y], near.at[y]) for y in range(strip)))
    first, second = jnp.zeros((1, c), F32), jnp.zeros((1, c), F32)
    for y in range(strip):
        copies[y].wait()
        v = near[y].astype(F32)
        first = first + jnp.sum(v, axis=0, keepdims=True)
        second = second + jnp.sum(v * v, axis=0, keepdims=True)
    pack_sums(first, second, out_ref)


def taps(lhs, w):
    return lax.dot_general(lhs, w, (((1,), (1,)), ((), ())), preferred_element_type=F32)


def columns(a):
    width, wide = a.shape
    c = wide // 3
    at = lax.broadcasted_iota(jnp.int32, (width, c), 0)
    left = pltpu.roll(a[:, :c], width - 1, 0)
    right = pltpu.roll(a[:, 2 * c :], 1, 0)
    left = jnp.where(at == width - 1, 0.0, left)
    right = jnp.where(at == 0, 0.0, right)
    return a[:, c : 2 * c] + left + right


def flat(w_ref, frame_tap, row_tap):
    c = w_ref.shape[-1]
    return w_ref[frame_tap, row_tap].reshape(3 * c, c)


def own_body(slab_ref, far_ref, acc_ref, w_ref, slab, sems):
    _, strip, _, _ = slab_ref.shape
    copies = fetch(
        sems, (slab_ref.at[0], slab), (far_ref.at[2], w_ref.at[2]),
        (far_ref.at[1], w_ref.at[1]), (far_ref.at[0], w_ref.at[0]),
    )
    copies[0].wait()
    copies[1].wait()
    for y in range(-1, strip + 1):
        rows = [(y + 1 - i, i) for i in range(3) if 0 <= y + 1 - i < strip]
        lhs = jnp.concatenate([slab[r] for r, _ in rows], axis=1)
        w = jnp.concatenate([flat(w_ref, 2, i) for _, i in rows], axis=1)
        acc_ref[y + 1] = columns(taps(lhs, w))
    copies[2].wait()
    copies[3].wait()


def border_body(
    xl_ref, dl_ref, le_ref, lo_ref, w_ref, acc_ref, out_ref, mate_ref, other_ref, xl, dl, le, lo, sems
):
    strip, _, _ = xl_ref.shape
    ends = (0, strip - 1)
    odd = lax.axis_index("rows") % 2
    copies = fetch(
        sems, *((xl_ref.at[r], xl.at[n]) for n, r in enumerate(ends)),
        *((le_ref.at[r], le.at[n]) for n, r in enumerate(ends)),
        *((lo_ref.at[r], lo.at[n]) for n, r in enumerate(ends)), (dl_ref, dl),
    )
    for copy in copies:
        copy.wait()
    lhs = [jnp.concatenate([xl[n] + dl[n], le[n] + lo[n]], axis=1) for n in range(2)]
    for i in (0, 2, 1):
        w = jnp.concatenate([flat(w_ref, 1, i), flat(w_ref, 0, i)], axis=1)
        for n, r in enumerate(ends):
            y = r - 1 + i
            value = acc_ref[y + 1] + columns(taps(lhs[n], w))
            if 0 <= y < strip:
                out_ref[y] = value
                continue
            value = value.astype(BF16)

            @pl.when(odd == (1 if y == -1 else 0))
            def _():
                mate_ref[...] = value

            @pl.when(odd == (0 if y == -1 else 1))
            def _():
                other_ref[...] = value


def inner_body(xl_ref, rl_ref, le_ref, lo_ref, w_ref, acc_ref, out_ref, xl, rl, le, lo, sems):
    strip = acc_ref.shape[0]
    copies = fetch(
        sems, (xl_ref.at[1 : strip - 1], xl), (rl_ref, rl), (le_ref.at[1 : strip - 1], le),
        (lo_ref.at[1 : strip - 1], lo),
    )
    for copy in copies:
        copy.wait()
    frames = [jnp.concatenate([xl[r] + rl[r], le[r] + lo[r]], axis=1) for r in range(strip - 2)]
    for y in range(strip):
        use = [(y + 1 - i, i) for i in range(3) if 1 <= y + 1 - i < strip - 1]
        lhs = jnp.concatenate([frames[r - 1] for r, _ in use], axis=1)
        w = jnp.concatenate([flat(w_ref, k, i) for _, i in use for k in (1, 0)], axis=1)
        out_ref[y] = acc_ref[y] + columns(taps(lhs, w))


def last_body(
    cells, acc_ref, mate_ref, other_ref, far_x_ref, gain_ref, bias_ref, got_ref,
    grad_ref, x_ref, params_ref, sums_ref, mate, other, gains, biases, got, sems,
):
    strip, _, c = acc_ref.shape
    odd = lax.axis_index("rows") % 2
    copies = fetch(
        sems, (got_ref, got), (gain_ref, gains), (bias_ref, biases), (mate_ref, mate), (other_ref, other),
        *((far_x_ref.at[0, y], x_ref.at[y]) for y in range(strip)),
    )
    for copy in copies[:3]:
        copy.wait()
    total = jnp.sum(got[...], axis=0) / cells
    centre = total[0:1]
    variance = jnp.maximum(total[1:2] - centre * centre, 0.0)
    inv_std = lax.rsqrt(variance + EPS)
    params_ref[0:1] = centre
    params_ref[1:2] = inv_std
    gain, bias = gains[...], biases[...]
    first, second = jnp.zeros((1, c), F32), jnp.zeros((1, c), F32)
    for copy in copies[3:]:
        copy.wait()
    for y in range(strip):
        value = acc_ref[y]
        if y in (0, strip - 1):
            from_mate = odd == (1 if y == 0 else 0)
            value = value + jnp.where(from_mate, mate[...].astype(F32), other[...].astype(F32))
        normed = (x_ref[y].astype(F32) - centre) * inv_std
        preact = normed * gain + bias
        logistic = jax.nn.sigmoid(preact)
        grad = value * (logistic * (1.0 + preact * (1.0 - logistic)) * gain)
        grad_ref[y] = grad
        first = first + jnp.sum(grad, axis=0, keepdims=True)
        second = second + jnp.sum(grad * normed, axis=0, keepdims=True)
    pack_sums(first, second, sums_ref)


def final_body(cells, grad_ref, x_ref, params_ref, sums_ref, out_ref, rows, sems):
    strip, _, _ = grad_ref.shape
    centre, inv_std = params_ref[0:1], params_ref[1:2]
    means = jnp.sum(sums_ref[...], axis=0) / cells
    total, cross = means[0:1], means[1:2]
    copies = []
    for y in range(strip):
        normed = (x_ref[y].astype(F32) - centre) * inv_std
        value = inv_std * (grad_ref[y] - total - normed * cross)
        rows[y] = value.astype(BF16)
        copies.append(pltpu.make_async_copy(rows.at[y], out_ref.at[0, y], sems.at[y]))
        copies[-1].start()
    for copy in copies:
        copy.wait()


def shards(inputs, cotangent, kernel, norm_gain, norm_bias):
    _, strip, width, c = inputs.shape
    frames, lines = lax.axis_size("frames"), lax.axis_size("rows")
    devices = frames * lines
    cells = float(devices * strip * width * (c // GROUPS))
    size = width * c
    tap = 2 * size * c * 3
    whole, pair, line = (strip, width, c), (strip - 2, width, c), (width, c)
    near = lambda shape, kind=F32: pltpu.VMEM(shape, kind)
    sums_shape = near((devices, 2, c))
    slab = cotangent[0]

    def move(value, pairs, axis="frames"):
        return lax.ppermute(value, axis, pairs)

    def swap(sums):
        return lax.all_to_all(sums, ("frames", "rows"), 0, 0, tiled=True)

    latest_odd = move(slab, [(i, i - 2) for i in range(3, frames, 2)])
    latest_even = move(slab, [(i, i - 2) for i in range(2, frames, 2)])
    later_x = move(slab, [(i, i - 1) for i in range(1, frames, 2)])
    ends = jnp.concatenate([slab[:1], slab[strip - 1 :]])
    later_ends = move(ends, [(i, i - 1) for i in range(2, frames, 2)])
    later_in = move(latest_even[1 : strip - 1], [(i, i + 1) for i in range(0, frames - 2, 2)])

    (sums,) = call(
        stats_body, [sums_shape], 8 * strip * size, 2 * strip * size, (inputs,), far=(0,),
        scratch=[near(whole, BF16), DMA((strip,))],
    )
    got = swap(sums)
    acc, w = call(
        own_body, [near((strip + 2, width, c)), near(kernel.shape, BF16)],
        tap * 3 * strip, 8 * 6 * size, (cotangent, kernel), far=(0, 1), scratch=[near(whole, BF16), DMA((4,))],
    )
    acc, mate, other = call(
        border_body, [near(whole), near(line, BF16), near(line, BF16)], tap * 12, 8 * 16 * size,
        (later_x, later_ends, latest_even, latest_odd, w, acc), near=(4, 5),
        scratch=[near((2, width, c), BF16)] * 4 + [DMA((7,))],
    )
    mate = move(mate, [(i, i ^ 1) for i in range(lines)], "rows")
    between = [(i, i + 1) for i in range(1, lines - 1, 2)]
    other = move(other, between + [(j, i) for i, j in between], "rows")
    (acc,) = call(
        inner_body, [near(whole)], tap * 12, 8 * 12 * size, (later_x, later_in, latest_even, latest_odd, w, acc),
        near=(4, 5), scratch=[near(pair, BF16)] * 4 + [DMA((4,))],
    )
    grad, x, params, sums = call(
        functools.partial(last_body, cells), [near(whole), near(whole, BF16), near((8, c)), sums_shape],
        40 * strip * size, 8 * 4 * size,
        (acc, mate, other, inputs, norm_gain.reshape(1, c), norm_bias.reshape(1, c), got),
        near=(0,), far=(3, 4, 5),
        scratch=[near(line, BF16), near(line, BF16), near((1, c)), near((1, c)), near((devices, 2, c)),
                 DMA((5 + strip,))],
    )
    sums = swap(sums)
    (out,) = call(
        functools.partial(final_body, cells), [jax.ShapeDtypeStruct(inputs.shape, BF16)],
        10 * strip * size, 8 * strip * size, (grad, x, params, sums), near=(0, 1, 2, 3),
        scratch=[near(whole, BF16), DMA((strip,))],
    )
    return out


def solution(mesh):
    return jax.shard_map(
        shards,
        mesh=mesh,
        in_specs=(P("frames", "rows", None, None), P("frames", "rows", None, None), P(), P(), P()),
        out_specs=P("frames", "rows", None, None),
        check_vma=False,
    )
```

```python
import functools
import jax
import jax.numpy as jnp
from jax import lax
from jax.experimental import pallas as pl
from jax.experimental.pallas import tpu as pltpu
from jax.sharding import PartitionSpec as P

GROUPS = 32
EPS = 1e-06
F32 = jnp.float32
BF16 = jnp.bfloat16
HIGH = lax.Precision.HIGHEST
DMA = pltpu.SemaphoreType.DMA
LIMIT = 24 * 1024 * 1024


def call(body, outs, flops, moved, args, near=(), far=(), scratch=()):
    spaces = [pltpu.VMEM if n in near else pltpu.HBM if n in far else None for n in range(len(args))]
    return pl.pallas_call(
        body,
        out_shape=outs,
        in_specs=[pl.BlockSpec(memory_space=m or pl.ANY) for m in spaces],
        out_specs=[
            pl.BlockSpec(memory_space=getattr(o, "memory_space", pltpu.HBM))
            for o in outs
        ],
        scratch_shapes=list(scratch),
        cost_estimate=pl.CostEstimate(flops=flops, bytes_accessed=moved, transcendentals=0),
        compiler_params=pltpu.CompilerParams(vmem_limit_bytes=LIMIT),
    )(*(v if m is None else pltpu.with_memory_space_constraint(v, m) for v, m in zip(args, spaces)))


def fetch(sems, *pairs):
    copies = [pltpu.make_async_copy(a, b, sems.at[n]) for n, (a, b) in enumerate(pairs)]
    for copy in copies:
        copy.start()
    return copies


def same_group(channels):
    per = channels // GROUPS
    one = lax.broadcasted_iota(jnp.int32, (channels, channels), 0) // per
    two = lax.broadcasted_iota(jnp.int32, (channels, channels), 1) // per
    return (one == two).astype(F32)


def pack_sums(first, second, out_ref):
    channels = first.shape[-1]
    row = lax.broadcasted_iota(jnp.int32, (8, channels), 0)
    both = jnp.where(row == 0, first, jnp.where(row == 1, second, 0.0))
    sums = jnp.dot(both, same_group(channels), precision=HIGH, preferred_element_type=F32)
    out_ref[...] = jnp.broadcast_to(sums[None, 0:2], out_ref.shape)


def cut_body(slab_ref, inner_ref, ends_ref, sems):
    strip = slab_ref.shape[1]
    for copy in fetch(
        sems, (slab_ref.at[0, 0], ends_ref.at[0]), (slab_ref.at[0, strip - 1], ends_ref.at[1]),
        (slab_ref.at[0, 1 : strip - 1], inner_ref),
    ):
        copy.wait()


def stats_body(x_ref, out_ref, near, sems):
    _, strip, _, c = x_ref.shape
    copies = fetch(sems, *((x_ref.at[0, y], near.at[y]) for y in range(strip)))
    first, second = jnp.zeros((1, c), F32), jnp.zeros((1, c), F32)
    for y in range(strip):
        copies[y].wait()
        v = near[y].astype(F32)
        first = first + jnp.sum(v, axis=0, keepdims=True)
        second = second + jnp.sum(v * v, axis=0, keepdims=True)
    pack_sums(first, second, out_ref)


def taps(lhs, w):
    return lax.dot_general(lhs, w, (((1,), (1,)), ((), ())), preferred_element_type=F32)


def columns(a):
    width, wide = a.shape
    c = wide // 3
    at = lax.broadcasted_iota(jnp.int32, (8, c), 0)
    left = pltpu.roll(a[:, :c], width - 1, 0)
    right = pltpu.roll(a[:, 2 * c :], 1, 0)
    left = jnp.concatenate([left[: width - 8], jnp.where(at == 7, 0.0, left[width - 8 :])], axis=0)
    right = jnp.concatenate([jnp.where(at == 0, 0.0, right[:8]), right[8:]], axis=0)
    return a[:, c : 2 * c] + left + right


def flat(w_ref, frame_tap, row_tap):
    c = w_ref.shape[-1]
    return w_ref[frame_tap, row_tap].reshape(3 * c, c)


def own_body(
    slab_ref, far_ref, gain_ref, bias_ref, acc_ref, gains_ref, biases_ref, slab, w_own, rows, sems, out_sems
):
    _, strip, _, c = slab_ref.shape
    copies = fetch(
        sems, (slab_ref.at[0], slab), (far_ref.at[2], w_own), (gain_ref, gains_ref), (bias_ref, biases_ref)
    )
    copies[0].wait()
    copies[1].wait()
    leaving = []
    for y in range(-1, strip + 1):
        use = [(y + 1 - i, i) for i in range(3) if 0 <= y + 1 - i < strip]
        lhs = jnp.concatenate([slab[r] for r, _ in use], axis=1)
        w = jnp.concatenate([w_own[i].reshape(3 * c, c) for _, i in use], axis=1)
        rows[y + 1] = columns(taps(lhs, w))
        leaving.append(pltpu.make_async_copy(rows.at[y + 1], acc_ref.at[y + 1], out_sems.at[y + 1]))
        leaving[-1].start()
    for copy in copies[2:] + leaving:
        copy.wait()


def load_body(far_ref, w_ref, sems):
    for copy in fetch(sems, *((far_ref.at[k], w_ref.at[k]) for k in range(2))):
        copy.wait()


def either(mine, start_odd, start_even):
    @pl.when(mine)
    def _():
        for copy in start_odd:
            copy.start()

    @pl.when(jnp.logical_not(mine))
    def _():
        for copy in start_even:
            copy.start()


def fetch_ends(side_ref, dl_ref, later, sems):
    top = side_ref.shape[0] - 1
    copy = pltpu.make_async_copy
    of_odd = [copy(dl_ref.at[n], later.at[n], sems.at[n]) for n in range(2)]
    of_even = [copy(side_ref.at[n * top], later.at[n], sems.at[n]) for n in range(2)]
    either(lax.axis_index("frames") % 2 == 1, of_odd, of_even)
    return of_odd


def edge_body(
    side_ref, dl_ref, le_ref, w_ref, acc_ref, mate_ref, other_ref, later_ref, latest_ref, leave, edges, sems
):
    strip = side_ref.shape[0]
    odd_line = lax.axis_index("rows") % 2
    of_odd = fetch_ends(side_ref, dl_ref, later_ref, sems)
    rest = fetch(
        sems.at[2:6], *((le_ref.at[n], latest_ref.at[n]) for n in range(2)),
        *((acc_ref.at[n * (strip + 1)], edges.at[n]) for n in range(2)),
    )
    for n in range(2):
        for one in (of_odd[n], rest[n], rest[2 + n]):
            one.wait()
        lhs = jnp.concatenate([later_ref[n], latest_ref[n]], axis=1)
        w = jnp.concatenate([flat(w_ref, 1, 2 * n), flat(w_ref, 0, 2 * n)], axis=1)
        leave[n] = (edges[n] + columns(taps(lhs, w))).astype(BF16)
    mate_ref[...] = leave[1 - odd_line]
    other_ref[...] = leave[odd_line]


def mid_body(
    cells, side_ref, dl_ref, le_ref, w_ref, far_acc_ref, far_x_ref, gains_ref, biases_ref, got_ref,
    acc_ref, factor_ref, x_ref, params_ref, later_ref, latest_ref, got, sems,
):
    strip = acc_ref.shape[0]
    top = strip - 1
    copies = fetch(
        sems.at[2 : 5 + strip], (got_ref, got), *((far_x_ref.at[0, y], x_ref.at[y]) for y in range(strip)),
        (far_acc_ref.at[1 : strip + 1], acc_ref), (le_ref, latest_ref),
    )
    copies += fetch_ends(side_ref, dl_ref, later_ref, sems)
    copies[0].wait()
    total = jnp.sum(got[...], axis=0) / cells
    centre = total[0:1]
    variance = jnp.maximum(total[1:2] - centre * centre, 0.0)
    inv_std = lax.rsqrt(variance + EPS)
    params_ref[0:1] = centre
    params_ref[1:2] = inv_std
    gain, bias = gains_ref[...], biases_ref[...]
    scale = inv_std * gain
    for copy in copies[1:]:
        copy.wait()
    for n, r in enumerate((0, top)):
        lhs = jnp.concatenate([later_ref[n], latest_ref[n]], axis=1)
        for i in range(3):
            y = r - 1 + i
            if 0 <= y < strip:
                w = jnp.concatenate([flat(w_ref, 1, i), flat(w_ref, 0, i)], axis=1)
                acc_ref[y] += columns(taps(lhs, w))
                preact = (x_ref[y].astype(F32) - centre) * scale + bias
                logistic = 0.5 + 0.5 * jnp.tanh(0.5 * preact)
                factor_ref[y] = logistic * (1.0 + preact * (1.0 - logistic)) * gain


def rest_body(
    side_ref, r1_ref, e1_ref, oi_ref, w_ref, acc_ref, factor_ref, x_ref, params_ref, mate_ref, other_ref,
    grad_ref, sums_ref, later, latest, mate, other, sems,
):
    strip, _, c = acc_ref.shape
    top = strip - 1
    odd_frame, odd_line = lax.axis_index("frames") % 2 == 1, lax.axis_index("rows") % 2
    copy = pltpu.make_async_copy
    of_odd = [copy(r1_ref, later, sems.at[0]), copy(oi_ref, latest, sems.at[1])]
    of_even = [copy(side_ref.at[1:top], later, sems.at[0]), copy(e1_ref, latest, sems.at[1])]
    either(odd_frame, of_odd, of_even)
    for one in of_odd + fetch(sems.at[2:4], (mate_ref, mate), (other_ref, other)):
        one.wait()
    centre, inv_std = params_ref[0:1], params_ref[1:2]
    frames = [jnp.concatenate([later[r], latest[r]], axis=1) for r in range(strip - 2)]
    first, second = jnp.zeros((1, c), F32), jnp.zeros((1, c), F32)
    for y in range(strip):
        use = [(y + 1 - i, i) for i in range(3) if 1 <= y + 1 - i < top]
        lhs = jnp.concatenate([frames[r - 1] for r, _ in use], axis=1)
        w = jnp.concatenate([flat(w_ref, k, i) for _, i in use for k in (1, 0)], axis=1)
        value = acc_ref[y] + columns(taps(lhs, w))
        if y in (0, top):
            from_mate = odd_line == (1 if y == 0 else 0)
            value = value + jnp.where(from_mate, mate[...].astype(F32), other[...].astype(F32))
        grad = value * factor_ref[y]
        grad_ref[y] = grad
        first = first + jnp.sum(grad, axis=0, keepdims=True)
        second = second + jnp.sum(grad * (x_ref[y].astype(F32) - centre), axis=0, keepdims=True)
    pack_sums(first, second * inv_std, sums_ref)


def final_body(cells, grad_ref, x_ref, params_ref, sums_ref, out_ref, rows, sems):
    strip = x_ref.shape[0]
    centre, inv_std = params_ref[0:1], params_ref[1:2]
    means = jnp.sum(sums_ref[...], axis=0) / cells
    total, cross = means[0:1], means[1:2]
    copies = []
    for y in range(strip):
        normed = (x_ref[y].astype(F32) - centre) * inv_std
        rows[y] = (inv_std * (grad_ref[y] - total - normed * cross)).astype(BF16)
        copies.append(pltpu.make_async_copy(rows.at[y], out_ref.at[0, y], sems.at[y]))
        copies[-1].start()
    for copy in copies:
        copy.wait()


def shards(inputs, cotangent, kernel, norm_gain, norm_bias):
    _, strip, width, c = inputs.shape
    frames, lines = lax.axis_size("frames"), lax.axis_size("rows")
    devices = frames * lines
    cells = float(devices * strip * width * (c // GROUPS))
    size = width * c
    tap = 2 * size * c * 3
    whole, pair, line = (strip, width, c), (strip - 2, width, c), (width, c)
    near = lambda shape, kind=F32: pltpu.VMEM(shape, kind)
    sums_shape = near((devices, 2, c))
    slab = cotangent[0]

    def move(value, pairs, axis="frames"):
        return lax.ppermute(value, axis, pairs)

    def swap(sums):
        return lax.all_to_all(sums, ("frames", "rows"), 0, 0, tiled=True)

    inner, ends = call(
        cut_body, [near(pair, BF16), near((2, width, c), BF16)], 0, 4 * strip * size, (cotangent,), far=(0,),
        scratch=[DMA((3,))],
    )
    evens = [(i, i - 1) for i in range(2, frames, 2)]
    direct = move(ends, evens)
    e1 = move(inner, [(i, i - 2) for i in range(2, frames, 2)])
    latest_ends = move(ends, [(i, i - 2) for i in range(2, frames)])
    later_x = move(slab, [(i, i - 1) for i in range(1, frames, 2)])
    odd_inner = move(inner, [(i, i - 2) for i in range(3, frames, 2)])
    r1 = move(e1, [(i, i + 1) for i in range(0, frames - 2, 2)])

    (sums,) = call(
        stats_body, [sums_shape], 8 * strip * size, 2 * strip * size, (inputs,), far=(0,),
        scratch=[near(whole, BF16), DMA((strip,))],
    )
    got = swap(sums)
    vec, two, row8 = near((1, c)), near((2, width, c), BF16), near((8, c))
    acc, gains, biases = call(
        own_body, [pltpu.HBM((strip + 2, width, c), F32), vec, vec],
        tap * 3 * strip, 8 * 6 * size, (cotangent, kernel, norm_gain.reshape(1, c), norm_bias.reshape(1, c)),
        far=(0, 1, 2, 3),
        scratch=[near(whole, BF16), near(kernel.shape[1:], BF16), near((strip + 2, width, c)), DMA((4,)),
                 DMA((strip + 2,))],
    )
    (w,) = call(
        load_body, [near((2,) + kernel.shape[1:], BF16)], 0, 4 * 18 * c * c, (kernel,), far=(0,),
        scratch=[DMA((2,))],
    )
    mate, other = call(
        edge_body, [near(line, BF16), near(line, BF16)], tap * 4, 8 * 8 * size,
        (later_x, direct, latest_ends, w, acc), near=(3,), far=(4,),
        scratch=[two, two, two, near((2, width, c)), DMA((6,))],
    )
    mate = move(mate, [(i, i ^ 1) for i in range(lines)], "rows")
    between = [(i, i + 1) for i in range(1, lines - 1, 2)]
    other = move(other, between + [(j, i) for i, j in between], "rows")
    acc, factor, x, params = call(
        functools.partial(mid_body, cells), [near(whole), near(whole), near(whole, BF16), row8],
        tap * 8, 8 * 10 * size,
        (later_x, direct, latest_ends, w, acc, inputs, gains, biases, got), near=(3, 6, 7), far=(4, 5),
        scratch=[two, two, near((devices, 2, c)), DMA((5 + strip,))],
    )
    grad, sums = call(
        rest_body, [near(whole), sums_shape], tap * 12, 8 * 12 * size,
        (later_x, r1, e1, odd_inner, w, acc, factor, x, params, mate, other), near=(4, 5, 6, 7, 8),
        scratch=[near(pair, BF16), near(pair, BF16), near(line, BF16), near(line, BF16), DMA((4,))],
    )
    sums = swap(sums)
    (out,) = call(
        functools.partial(final_body, cells), [jax.ShapeDtypeStruct(inputs.shape, BF16)],
        10 * strip * size, 8 * strip * size, (grad, x, params, sums), near=(0, 1, 2, 3),
        scratch=[near(whole, BF16), DMA((strip,))],
    )
    return out


def solution(mesh):
    return jax.shard_map(
        shards,
        mesh=mesh,
        in_specs=(P("frames", "rows", None, None), P("frames", "rows", None, None), P(), P(), P()),
        out_specs=P("frames", "rows", None, None),
        check_vma=False,
    )
```

```python
import functools
import jax
import jax.numpy as jnp
from jax import lax
from jax.experimental import pallas as pl
from jax.experimental.pallas import tpu as pltpu
from jax.sharding import PartitionSpec as P

GROUPS = 32
EPS = 1e-06
F32 = jnp.float32
BF16 = jnp.bfloat16
HIGH = lax.Precision.HIGHEST
DMA = pltpu.SemaphoreType.DMA
LIMIT = 24 * 1024 * 1024


def call(body, outs, flops, moved, args, near=(), far=(), scratch=()):
    spaces = [pltpu.VMEM if n in near else pltpu.HBM if n in far else None for n in range(len(args))]
    return pl.pallas_call(
        body,
        out_shape=outs,
        in_specs=[pl.BlockSpec(memory_space=m or pl.ANY) for m in spaces],
        out_specs=[
            pl.BlockSpec(memory_space=getattr(o, "memory_space", pltpu.HBM))
            for o in outs
        ],
        scratch_shapes=list(scratch),
        cost_estimate=pl.CostEstimate(flops=flops, bytes_accessed=moved, transcendentals=0),
        compiler_params=pltpu.CompilerParams(vmem_limit_bytes=LIMIT),
    )(*(v if m is None else pltpu.with_memory_space_constraint(v, m) for v, m in zip(args, spaces)))


def fetch(sems, *pairs):
    copies = [pltpu.make_async_copy(a, b, sems.at[n]) for n, (a, b) in enumerate(pairs)]
    for copy in copies:
        copy.start()
    return copies


def same_group(channels):
    per = channels // GROUPS
    one = lax.broadcasted_iota(jnp.int32, (channels, channels), 0) // per
    two = lax.broadcasted_iota(jnp.int32, (channels, channels), 1) // per
    return (one == two).astype(F32)


def pack_sums(first, second, out_ref):
    channels = first.shape[-1]
    row = lax.broadcasted_iota(jnp.int32, (8, channels), 0)
    both = jnp.where(row == 0, first, jnp.where(row == 1, second, 0.0))
    sums = jnp.dot(both, same_group(channels), precision=HIGH, preferred_element_type=F32)
    out_ref[...] = jnp.broadcast_to(sums[None, 0:2], out_ref.shape)


def cut_body(slab_ref, inner_ref, ends_ref, rows, sems, out_sems):
    strip = slab_ref.shape[1]
    copies = fetch(sems, *((slab_ref.at[0, y], rows.at[y]) for y in range(strip)))
    leaving = []
    for y in range(strip):
        to = ends_ref.at[min(y, 1)] if y in (0, strip - 1) else inner_ref.at[y - 1]
        copies[y].wait()
        leaving.append(pltpu.make_async_copy(rows.at[y], to, out_sems.at[y]))
        leaving[-1].start()
    for copy in leaving:
        copy.wait()


def taps(lhs, w):
    return lax.dot_general(lhs, w, (((1,), (1,)), ((), ())), preferred_element_type=F32)


def columns(a):
    width, wide = a.shape
    c = wide // 3
    at = lax.broadcasted_iota(jnp.int32, (8, c), 0)
    left = pltpu.roll(a[:, :c], width - 1, 0)
    right = pltpu.roll(a[:, 2 * c :], 1, 0)
    left = jnp.concatenate([left[: width - 8], jnp.where(at == 7, 0.0, left[width - 8 :])], axis=0)
    right = jnp.concatenate([jnp.where(at == 0, 0.0, right[:8]), right[8:]], axis=0)
    return a[:, c : 2 * c] + left + right


def flat(w_ref, frame_tap, row_tap):
    c = w_ref.shape[-1]
    return w_ref[frame_tap, row_tap].reshape(3 * c, c)


def own_body(
    slab_ref, far_ref, far_x_ref, gain_ref, bias_ref, acc_ref, w_ref, gains_ref, biases_ref, sums_ref,
    slab, w_own, x, rows, sems, out_sems,
):
    _, strip, _, c = slab_ref.shape
    copies = fetch(
        sems, (slab_ref.at[0], slab), (far_ref.at[2], w_own), (far_x_ref.at[0], x), (far_ref.at[1], w_ref.at[1]),
        (far_ref.at[0], w_ref.at[0]), (gain_ref, gains_ref), (bias_ref, biases_ref),
    )
    for copy in copies[:3]:
        copy.wait()
    first, second = jnp.zeros((1, c), F32), jnp.zeros((1, c), F32)
    leaving = []
    for y in range(-1, strip + 1):
        use = [(y + 1 - i, i) for i in range(3) if 0 <= y + 1 - i < strip]
        lhs = jnp.concatenate([slab[r] for r, _ in use], axis=1)
        w = jnp.concatenate([w_own[i].reshape(3 * c, c) for _, i in use], axis=1)
        rows[y + 1] = columns(taps(lhs, w))
        leaving.append(pltpu.make_async_copy(rows.at[y + 1], acc_ref.at[y + 1], out_sems.at[y + 1]))
        leaving[-1].start()
        if 0 <= y < strip:
            v = x[y].astype(F32)
            first = first + jnp.sum(v, axis=0, keepdims=True)
            second = second + jnp.sum(v * v, axis=0, keepdims=True)
    pack_sums(first, second, sums_ref)
    for copy in copies[3:] + leaving:
        copy.wait()


def either(mine, start_odd, start_even):
    @pl.when(mine)
    def _():
        for copy in start_odd:
            copy.start()

    @pl.when(jnp.logical_not(mine))
    def _():
        for copy in start_even:
            copy.start()


def edge_body(
    la_ref, le_ref, w_ref, acc_ref, mate_ref, other_ref, later_ref, latest_ref, leave, edges, sems
):
    last = acc_ref.shape[0] - 1
    odd_line = lax.axis_index("rows") % 2
    for copy in fetch(
        sems, (la_ref, later_ref), (le_ref, latest_ref), (acc_ref.at[0], edges.at[0]), (acc_ref.at[last], edges.at[1])
    ):
        copy.wait()
    for n in range(2):
        lhs = jnp.concatenate([later_ref[n], latest_ref[n]], axis=1)
        w = jnp.concatenate([flat(w_ref, 1, 2 * n), flat(w_ref, 0, 2 * n)], axis=1)
        leave[n] = (edges[n] + columns(taps(lhs, w))).astype(BF16)
    mate_ref[...] = leave[1 - odd_line]
    other_ref[...] = leave[odd_line]


def mid_body(
    cells, la_ref, le_ref, w_ref, far_acc_ref, far_x_ref, gains_ref, biases_ref, got_ref,
    acc_ref, factor_ref, x_ref, params_ref, later_ref, latest_ref, got, sems,
):
    strip = acc_ref.shape[0]
    top = strip - 1
    copies = fetch(
        sems, (got_ref, got), *((far_x_ref.at[0, y], x_ref.at[y]) for y in range(strip)),
        (far_acc_ref.at[1 : strip + 1], acc_ref), (la_ref, later_ref), (le_ref, latest_ref),
    )
    copies[0].wait()
    total = jnp.sum(got[...], axis=0) / cells
    centre = total[0:1]
    variance = jnp.maximum(total[1:2] - centre * centre, 0.0)
    inv_std = lax.rsqrt(variance + EPS)
    params_ref[0:1] = centre
    params_ref[1:2] = inv_std
    gain, bias = gains_ref[...], biases_ref[...]
    scale = inv_std * gain
    for copy in copies[1:]:
        copy.wait()
    for n, r in enumerate((0, top)):
        lhs = jnp.concatenate([later_ref[n], latest_ref[n]], axis=1)
        for i in range(3):
            y = r - 1 + i
            if 0 <= y < strip:
                w = jnp.concatenate([flat(w_ref, 1, i), flat(w_ref, 0, i)], axis=1)
                acc_ref[y] += columns(taps(lhs, w))
                preact = (x_ref[y].astype(F32) - centre) * scale + bias
                logistic = 0.5 + 0.5 * jnp.tanh(0.5 * preact)
                factor_ref[y] = logistic * (1.0 + preact * (1.0 - logistic)) * gain


def rest_body(
    side_ref, r1_ref, e1_ref, oi_ref, w_ref, acc_ref, factor_ref, x_ref, params_ref, mate_ref, other_ref,
    grad_ref, sums_ref, later, latest, mate, other, sems,
):
    strip, _, c = acc_ref.shape
    top = strip - 1
    odd_frame, odd_line = lax.axis_index("frames") % 2 == 1, lax.axis_index("rows") % 2
    copy = pltpu.make_async_copy
    of_odd = [copy(r1_ref, later, sems.at[0]), copy(oi_ref, latest, sems.at[1])]
    of_even = [copy(side_ref, later, sems.at[0]), copy(e1_ref, latest, sems.at[1])]
    either(odd_frame, of_odd, of_even)
    for one in of_odd + fetch(sems.at[2:4], (mate_ref, mate), (other_ref, other)):
        one.wait()
    centre, inv_std = params_ref[0:1], params_ref[1:2]
    frames = [jnp.concatenate([later[r], latest[r]], axis=1) for r in range(strip - 2)]
    first, second = jnp.zeros((1, c), F32), jnp.zeros((1, c), F32)
    for y in range(strip):
        use = [(y + 1 - i, i) for i in range(3) if 1 <= y + 1 - i < top]
        lhs = jnp.concatenate([frames[r - 1] for r, _ in use], axis=1)
        w = jnp.concatenate([flat(w_ref, k, i) for _, i in use for k in (1, 0)], axis=1)
        value = acc_ref[y] + columns(taps(lhs, w))
        if y in (0, top):
            from_mate = odd_line == (1 if y == 0 else 0)
            value = value + jnp.where(from_mate, mate[...].astype(F32), other[...].astype(F32))
        grad = value * factor_ref[y]
        grad_ref[y] = grad
        first = first + jnp.sum(grad, axis=0, keepdims=True)
        second = second + jnp.sum(grad * (x_ref[y].astype(F32) - centre), axis=0, keepdims=True)
    pack_sums(first, second * inv_std, sums_ref)


def final_body(cells, grad_ref, x_ref, params_ref, sums_ref, out_ref, rows, sems):
    strip = x_ref.shape[0]
    centre, inv_std = params_ref[0:1], params_ref[1:2]
    means = jnp.sum(sums_ref[...], axis=0) / cells
    total, cross = means[0:1], means[1:2]
    copies = []
    for y in range(strip):
        normed = (x_ref[y].astype(F32) - centre) * inv_std
        rows[y] = (inv_std * (grad_ref[y] - total - normed * cross)).astype(BF16)
        copies.append(pltpu.make_async_copy(rows.at[y], out_ref.at[0, y], sems.at[y]))
        copies[-1].start()
    for copy in copies:
        copy.wait()


def shards(inputs, cotangent, kernel, norm_gain, norm_bias):
    _, strip, width, c = inputs.shape
    frames, lines = lax.axis_size("frames"), lax.axis_size("rows")
    devices = frames * lines
    cells = float(devices * strip * width * (c // GROUPS))
    size = width * c
    tap = 2 * size * c * 3
    whole, pair, line = (strip, width, c), (strip - 2, width, c), (width, c)
    near = lambda shape, kind=F32: pltpu.VMEM(shape, kind)
    sums_shape = near((devices, 2, c))

    def move(value, pairs, axis="frames"):
        return lax.ppermute(value, axis, pairs)

    def swap(sums):
        return lax.all_to_all(sums, ("frames", "rows"), 0, 0, tiled=True)

    inner, ends = call(
        cut_body, [pltpu.HBM(pair, BF16), pltpu.HBM((2, width, c), BF16)], 0, 4 * strip * size, (cotangent,),
        far=(0,), scratch=[near(whole, BF16), DMA((strip,)), DMA((strip,))],
    )
    twos = [(i, i - 2) for i in range(2, frames)]
    e1 = move(inner, [p for p in twos if p[0] % 2 == 0])
    latest = move(ends, twos)
    later = move(ends, [(i, i - 1) for i in range(1, frames)])
    side = move(inner, [(i, i - 1) for i in range(1, frames, 2)])
    odd_inner = move(inner, [p for p in twos if p[0] % 2 == 1])
    r1 = move(e1, [(i, i + 1) for i in range(0, frames - 2, 2)])

    vec, two, row8 = near((1, c)), near((2, width, c), BF16), near((8, c))
    acc, w, gains, biases, sums = call(
        own_body,
        [pltpu.HBM((strip + 2, width, c), F32), near((2,) + kernel.shape[1:], BF16), vec, vec, sums_shape],
        tap * 3 * strip, 8 * 6 * size,
        (cotangent, kernel, inputs, norm_gain.reshape(1, c), norm_bias.reshape(1, c)), far=(0, 1, 2, 3, 4),
        scratch=[near(whole, BF16), near(kernel.shape[1:], BF16), near(whole, BF16),
                 near((strip + 2, width, c)), DMA((7,)), DMA((strip + 2,))],
    )
    got = swap(sums)
    mate, other = call(
        edge_body, [near(line, BF16), near(line, BF16)], tap * 4, 8 * 8 * size,
        (later, latest, w, acc), near=(2,), far=(3,),
        scratch=[two, two, two, near((2, width, c)), DMA((4,))],
    )
    mate = move(mate, [(i, i ^ 1) for i in range(lines)], "rows")
    between = [(i, i + 1) for i in range(1, lines - 1, 2)]
    other = move(other, between + [(j, i) for i, j in between], "rows")
    acc, factor, x, params = call(
        functools.partial(mid_body, cells), [near(whole), near(whole), near(whole, BF16), row8],
        tap * 8, 8 * 10 * size,
        (later, latest, w, acc, inputs, gains, biases, got), near=(2, 5, 6), far=(3, 4),
        scratch=[two, two, near((devices, 2, c)), DMA((5 + strip,))],
    )
    grad, sums = call(
        rest_body, [near(whole), sums_shape], tap * 12, 8 * 12 * size,
        (side, r1, e1, odd_inner, w, acc, factor, x, params, mate, other), near=(4, 5, 6, 7, 8),
        scratch=[near(pair, BF16), near(pair, BF16), near(line, BF16), near(line, BF16), DMA((4,))],
    )
    sums = swap(sums)
    (out,) = call(
        functools.partial(final_body, cells), [jax.ShapeDtypeStruct(inputs.shape, BF16)],
        10 * strip * size, 8 * strip * size, (grad, x, params, sums), near=(0, 1, 2, 3),
        scratch=[near(whole, BF16), DMA((strip,))],
    )
    return out


def solution(mesh):
    return jax.shard_map(
        shards,
        mesh=mesh,
        in_specs=(P("frames", "rows", None, None), P("frames", "rows", None, None), P(), P(), P()),
        out_specs=P("frames", "rows", None, None),
        check_vma=False,
    )
```
